768 devices in a mesh: ctx: 96 (over z_lo, y, x), kvh: 8 (over z_hi, core).
Axes of the slice: x: 4, y: 8, z: 12 (z_hi: 4, z_lo: 3; z = z_hi * 3 + z_lo), core: 2. Of those that a mesh axis runs over, the one named last changes fastest.
Arguments:
- queries: float32 [96, 256, 64, 128], P('ctx', None, 'kvh'), may hold values from -64 to 64
- cache_keys: float32 [8, 49152, 128], P('kvh', 'ctx'), may hold values from -16 to 16
- cache_values: float32 [8, 49152, 128], P('kvh', 'ctx'), may hold values from -6 to 6
- bounds: int32 [96, 3], replicated, may hold values from 0 to 2048, as said below
Outputs:
- attended: float32 [96, 256, 64, 128], P('ctx', None, 'kvh')
The draws below stay inside these ranges and needn't reach their ends.
Inputs may be any that keep to these rules, and one draw needn't show every extreme that they name: bounds[b] = (s, w, l) with 2 <= s <= 64, 0 <= w < 256, 1792 < l <= 2048; block 0 has s = 64, w = 0, l = 2048.
All inputs are finite; a program needn't handle non-finite values.
Results may differ from the reference program's by a relative error of at most 0.0003.
Values sent between devices are 32-bit elements; how exact they have to be, the bound alone decides.
A program may use at most 32 MiB of HBM per device.

```python
import math
import jax
import jax.numpy as jnp
from jax import lax

HEADS = 64
KVH = 8
HD = 128
QB = 256
ROWS = 512
SINK = 64
BLOCKS = 96
TOTAL = 49152
N_CTX = 96


def shared_keys(key):
    keys = jax.random.normal(jax.random.fold_in(key, 7), (KVH, TOTAL, HD), jnp.float32)
    return jnp.clip(keys, -16.0, 16.0)


def draw_cache_keys(key, part):
    return shared_keys(key)


def draw_queries(key, part):
    values = 2.0 * jax.random.normal(jax.random.fold_in(key, 13), (BLOCKS, QB, HEADS, HD), jnp.float32)
    return jnp.clip(values, -64.0, 64.0)


def draw_bounds(key, part):
    sink_end = jax.random.randint(jax.random.fold_in(key, 21), (BLOCKS,), 2, SINK + 1)
    window_start = jax.random.randint(jax.random.fold_in(key, 22), (BLOCKS,), 0, ROWS // 2)
    valid_end = 4 * ROWS - jax.random.randint(jax.random.fold_in(key, 23), (BLOCKS,), 0, ROWS // 2)
    sink_end = sink_end.at[0].set(SINK)
    window_start = window_start.at[0].set(0)
    valid_end = valid_end.at[0].set(4 * ROWS)
    return jnp.stack([sink_end, window_start, valid_end], axis=1).astype(jnp.int32)


def levels(rng, shape, pieces, least, top_value):
    def one(position, blocks):
        draws = jax.random.uniform(jax.random.fold_in(jax.random.fold_in(rng, 6), position), (blocks,), jnp.float32, least / len(pieces), top_value / len(pieces))
        return jnp.repeat(jnp.exp(draws), shape[position] // blocks).reshape((-1,) + (1,) * (len(shape) - position - 1))

    factor_of = one(*pieces[0])
    for cut in pieces[1:]:
        factor_of = factor_of * one(*cut)
    return factor_of


def normal_values(key, shape, deviation, most, shards=(), held_as=jnp.bfloat16):
    drawn = deviation * jax.random.normal(key, shape, jnp.float32)
    if shards:
        drawn = drawn * levels(key, shape, shards, -0.22, 0.18)
    return jnp.clip(drawn, -most, most).astype(held_as)


def setup_inputs(seed: int = 0) -> dict:
    key_of = jax.random.split(jax.random.key(seed), 5)
    return {
        "queries": draw_queries(jax.random.fold_in(key_of[4], 71), 0),
        "cache_keys": draw_cache_keys(jax.random.fold_in(key_of[4], 71), 0),
        "cache_values": normal_values(key_of[2], (KVH, TOTAL, HD), 1.0, 6.0, ((0, 8), (1, 96)), jnp.float32),
        "bounds": draw_bounds(jax.random.fold_in(key_of[4], 71), 0),
    }


NEG = -1e+30

def reference(queries, cache_keys, cache_values, bounds):
    total = ROWS * N_CTX
    group = HEADS // KVH
    scale = 1.0 / math.sqrt(HD)
    ext_keys = jnp.concatenate([cache_keys, cache_keys[:, :4 * ROWS]], axis=1)
    ext_values = jnp.concatenate([cache_values, cache_values[:, :4 * ROWS]], axis=1)

    def one(block):
        query = lax.dynamic_index_in_dim(queries, block, 0, keepdims=False).reshape(QB, KVH, group, HD)
        limits = lax.dynamic_index_in_dim(bounds, block, 0, keepdims=False)
        start = (block * ROWS).astype(jnp.int32)
        span_keys = lax.dynamic_slice_in_dim(ext_keys, start, 4 * ROWS, 1)
        span_values = lax.dynamic_slice_in_dim(ext_values, start, 4 * ROWS, 1)
        keys = jnp.concatenate([cache_keys[:, :SINK], span_keys], axis=1)
        values = jnp.concatenate([cache_values[:, :SINK], span_values], axis=1)
        offsets = jnp.arange(4 * ROWS, dtype=jnp.int32)
        span_mask = (offsets >= limits[1]) & (offsets < limits[2])
        slots = jnp.arange(SINK, dtype=jnp.int32)
        rel = (slots - start) % total
        sink_mask = (slots < limits[0]) & jnp.logical_not((rel >= limits[1]) & (rel < limits[2]))
        mask = jnp.concatenate([sink_mask, span_mask])
        scores = jnp.einsum('qkgd,ksd->kgqs', query, keys, precision=lax.Precision.HIGHEST) * scale
        masked = jnp.where(mask, scores, NEG)
        top = lax.optimization_barrier(jnp.max(masked, axis=-1, keepdims=True))
        weights = jnp.where(mask, jnp.exp(masked - top), 0.0)
        totals = lax.optimization_barrier(jnp.sum(weights, axis=-1))
        mixed = jnp.einsum('kgqs,ksd->kgqd', weights, values, precision=lax.Precision.HIGHEST)
        mixed = mixed / totals[..., None]
        return jnp.transpose(mixed, (2, 0, 1, 3)).reshape(QB, HEADS, HD)
    return lax.map(one, jnp.arange(BLOCKS, dtype=jnp.int32))
```

```python
import math

import jax
import jax.numpy as jnp
from jax import lax
from jax.experimental import pallas as pl
from jax.experimental.pallas import tpu as pltpu
from jax.sharding import PartitionSpec as P

SINK = 64
NEG = -1e30
NT = (((1,), (1,)), ((), ()))
NN = (((1,), (0,)), ((), ()))
F32, BF16 = jnp.float32, jnp.bfloat16
XS = 4
PLANE = 32

NEAR1, TRANSIT, NEAR3, FAR_A, FAR_B, SINKS, RELAY = 0, 4, 8, 12, 14, 16, 18
SINK_SENDS = 22


def split(x):
    high = x.astype(BF16)
    return high, (x - high.astype(F32)).astype(BF16)


def kernel(rows, count, bounds, q_hbm, k_hbm, v_hbm, o_ref, q_raw, kbuf, vbuf, ksink, vsink,
           qcat, kcat, klow, vcat, top, total, mixed, ssem, rsem, lsem):
    half, queries, size = rows // 2, q_hbm.shape[0], q_hbm.shape[1]
    b = lax.axis_index("ctx")
    x = lax.rem(b, XS)
    at = lambda d: lax.rem(b + d + count, count)

    def remote(src, dst, send, recv, target):
        return pltpu.make_async_remote_copy(
            src_ref=src, dst_ref=dst, send_sem=ssem.at[send], recv_sem=rsem.at[recv],
            device_id={"ctx": target}, device_id_type=pl.DeviceIdType.MESH)

    local = [
        pltpu.make_async_copy(q_hbm, q_raw, lsem.at[0]),
        pltpu.make_async_copy(k_hbm, kbuf.at[0], lsem.at[1]),
        pltpu.make_async_copy(v_hbm, vbuf.at[0], lsem.at[2]),
    ]
    for copy in local:
        copy.start()

    barrier = pltpu.get_barrier_semaphore()
    for d in (1, -1, 3, -3, 4, -4):
        pl.semaphore_signal(barrier, inc=1, device_id={"ctx": at(d)}, device_id_type=pl.DeviceIdType.MESH)
    low = lax.rem(b, PLANE)
    sink_source = jnp.where(b < XS, 0, jnp.where(b < PLANE, x, jnp.where(low < XS, low + XS, low)))

    @pl.when(b > 0)
    def _():
        pl.semaphore_signal(barrier, inc=1, device_id={"ctx": sink_source}, device_id_type=pl.DeviceIdType.MESH)

    ys = PLANE // XS - 1
    zs = count // PLANE - 1
    sink_targets = jnp.where(
        b == 0, ys + XS - 1, jnp.where(b < XS, ys, jnp.where(b < 2 * XS, 2 * zs, jnp.where(b < PLANE, zs, 0))))
    pl.semaphore_wait(barrier, 6 + sink_targets)

    def sink_copies(from_input, number, target):
        src = (k_hbm.at[0:SINK], v_hbm.at[0:SINK]) if from_input else (ksink.at[0:SINK], vsink.at[0:SINK])
        dst = (ksink.at[0:SINK], vsink.at[0:SINK])
        return [remote(src[i], dst[i], SINK_SENDS + 2 * number + i, SINKS + i, target) for i in range(2)]

    root_sends = [c for d in range(1, XS) for c in sink_copies(True, d - 1, d)]
    root_sends += [c for d in range(1, ys + 1) for c in sink_copies(True, XS - 2 + d, d * XS)]
    head_sends = [c for d in range(1, ys + 1) for c in sink_copies(False, d - 1, b + d * XS)]
    plane_sends = [c for d in range(1, zs + 1) for c in sink_copies(False, d - 1, b + d * PLANE)]
    extra_sends = [c for d in range(1, zs + 1) for c in sink_copies(False, zs + d - 1, b + d * PLANE - XS)]
    sink_in = [remote(ksink.at[0:SINK], ksink.at[0:SINK], SINK_SENDS, SINKS, at(1)),
               remote(vsink.at[0:SINK], vsink.at[0:SINK], SINK_SENDS, SINKS + 1, at(1))]
    own_sink = [pltpu.make_async_copy(k_hbm.at[0:SINK], ksink.at[0:SINK], lsem.at[3]),
                pltpu.make_async_copy(v_hbm.at[0:SINK], vsink.at[0:SINK], lsem.at[4])]

    @pl.when(b == 0)
    def _():
        for copy in own_sink + root_sends:
            copy.start()

    first, last = x == 0, x == XS - 1
    slot1 = jnp.where(first, 4, 1)
    sem1 = jnp.where(first, TRANSIT, NEAR1)
    target1 = jnp.where(first, at(3), at(-1))
    parts = lambda slot, off: (kbuf.at[slot, pl.ds(off, half)], vbuf.at[slot, pl.ds(off, half)])
    hbm_parts = lambda off: (k_hbm.at[pl.ds(off, half)], v_hbm.at[pl.ds(off, half)])
    near1, near3, relay, far_a, far_b = [], [], [], [], []
    for h in range(2):
        for i in range(2):
            j = 2 * h + i
            off1, off3 = h * half, (1 - h) * half
            near1.append(remote(hbm_parts(off1)[i], parts(slot1, off1)[i], NEAR1 + j, sem1 + j, target1))
            near3.append(remote(hbm_parts(off3)[i], parts(3, off3)[i], NEAR3 + j, NEAR3 + j, at(-3)))
            relay.append(remote(parts(4, off1)[i], parts(1, off1)[i], RELAY + j, NEAR1 + j, at(-4)))
    for i in range(2):
        far_a.append(remote(parts(1, 0)[i], parts(2, 0)[i], FAR_A + i, FAR_A + i, at(-1)))
        far_b.append(remote(parts(3, half)[i], parts(2, half)[i], FAR_B + i, FAR_B + i, at(1)))
    for j in range(4):
        near1[j].start()
        near3[j].start()
    near1_in = [remote(parts(1, (j // 2) * half)[j % 2], parts(1, (j // 2) * half)[j % 2], NEAR1 + j, NEAR1 + j, at(-1))
                for j in range(4)]
    transit_in = [remote(parts(4, (j // 2) * half)[j % 2], parts(4, (j // 2) * half)[j % 2], NEAR1 + j, TRANSIT + j, at(-1))
                  for j in range(4)]

    for copy in local:
        copy.wait()
    scale = math.log2(math.e) / math.sqrt(size)
    step = 256

    @pl.loop(0, queries // step)
    def _(i):
        at_rows = pl.ds(pl.multiple_of(i * step, step), step)
        high, rest = split(q_raw[at_rows, :] * scale)
        qcat[at_rows, 0:size] = high
        qcat[at_rows, size:2 * size] = rest
        top[at_rows, :] = jnp.full((step, size), NEG, F32)
        total[at_rows, :] = jnp.zeros((step, size), F32)
        mixed[at_rows, :] = jnp.zeros((step, size), F32)

    ksink[SINK:, :] = jnp.zeros((128 - SINK, size), F32)
    vsink[SINK:, :] = jnp.zeros((128 - SINK, size), F32)
    sink_end, lower, upper = bounds[0, b], bounds[1, b], bounds[2, b]
    block = 512

    def piece(keys, values, bias):
        n = keys.shape[0]
        high, rest = split(keys)
        kcat[0:n, 0:size] = high
        kcat[0:n, size:2 * size] = high
        klow[0:n, :] = rest
        high, rest = split(values)
        vcat[0:n, 0:size] = high
        vcat[0:n, size:2 * size] = rest

        @pl.loop(0, queries // block)
        def _(i):
            at_rows = pl.ds(pl.multiple_of(i * block, block), block)
            q = qcat[at_rows, :]
            s = lax.dot_general(q, kcat[0:n, :], NT, preferred_element_type=F32)
            s += lax.dot_general(q[:, :size], klow[0:n, :], NT, preferred_element_type=F32)
            s += bias
            before = top[at_rows, :]
            now = jnp.maximum(before, jnp.max(s, axis=1, keepdims=True))
            decay = jnp.exp2(before - now)
            p = jnp.exp2(s - jnp.concatenate([now] * (n // 128), axis=1))
            summed = p[:, 0:128]
            for t in range(1, n // 128):
                summed = summed + p[:, t * 128:(t + 1) * 128]
            high, rest = split(p)
            out = lax.dot_general(high, vcat[0:n, :], NN, preferred_element_type=F32)
            low = lax.dot_general(rest, vcat[0:n, 0:size], NN, preferred_element_type=F32)
            top[at_rows, :] = now
            total[at_rows, :] = total[at_rows, :] * decay + summed
            mixed[at_rows, :] = mixed[at_rows, :] * decay + (out[:, :size] + out[:, size:] + low)

    @pl.loop(0, 8)
    def _(i):
        slot = jnp.where(i < 2, 0, jnp.where(i > 5, 2, jnp.where(lax.rem(i, 2) == 0, 3, 1)))
        upper_half = (i == 1) | (i == 2) | (i == 5) | (i == 6)
        off = pl.multiple_of(jnp.where(upper_half, half, 0), half)

        @pl.when((i == 1) & (b > 0) & (b < XS))
        def _():
            for copy in sink_in:
                copy.wait_recv()
            for copy in head_sends:
                copy.start()

        @pl.when(i == 2)
        def _():
            @pl.when(last)
            def _():
                transit_in[0].wait_recv()
                relay[0].start()

            for j in range(2):
                near3[j].wait_recv()
                far_b[j].start()

        @pl.when(i == 3)
        def _():
            @pl.when(last)
            def _():
                transit_in[1].wait_recv()
                relay[1].start()

            for j in range(2):
                near1_in[j].wait_recv()
                far_a[j].start()

        @pl.when(i == 4)
        def _():
            @pl.when((b >= XS) & (b < PLANE))
            def _():
                for copy in sink_in:
                    copy.wait_recv()
                for copy in plane_sends:
                    copy.start()

                @pl.when(b < 2 * XS)
                def _():
                    for copy in extra_sends:
                        copy.start()

            @pl.when(last)
            def _():
                for j in range(2, 4):
                    transit_in[j].wait_recv()
                    relay[j].start()

            for j in range(2, 4):
                near3[j].wait_recv()

        @pl.when(i == 5)
        def _():
            for j in range(2, 4):
                near1_in[j].wait_recv()

        @pl.when(i == 6)
        def _():
            for j in range(2):
                far_b[j].wait_recv()

        @pl.when(i == 7)
        def _():
            for j in range(2):
                far_a[j].wait_recv()

        offsets = slot * rows + off + lax.broadcasted_iota(jnp.int32, (1, half), 1)
        seen = (offsets >= lower) & (offsets < upper)
        piece(kbuf[slot, pl.ds(off, half), :], vbuf[slot, pl.ds(off, half), :], jnp.where(seen, 0.0, NEG))

    @pl.when(b == 0)
    def _():
        for copy in own_sink:
            copy.wait()

    @pl.when(b >= PLANE)
    def _():
        for copy in sink_in:
            copy.wait_recv()

    slots = lax.broadcasted_iota(jnp.int32, (1, 128), 1)
    place = slots - b * rows
    place = jnp.where(place < 0, place + rows * count, place)
    seen = (slots < sink_end) & jnp.logical_not((place >= lower) & (place < upper))
    piece(ksink[...], vsink[...], jnp.where(seen, 0.0, NEG))

    @pl.loop(0, queries // step)
    def _(i):
        at_rows = pl.ds(pl.multiple_of(i * step, step), step)
        o_ref[at_rows, :] = mixed[at_rows, :] / jnp.sum(total[at_rows, :], axis=1, keepdims=True)

    for copy in near1 + near3 + far_a + far_b:
        copy.wait_send()

    @pl.when(last)
    def _():
        for copy in relay:
            copy.wait_send()

    @pl.when(b == 0)
    def _():
        for copy in root_sends:
            copy.wait_send()

    @pl.when((b > 0) & (b < XS))
    def _():
        for copy in head_sends:
            copy.wait_send()

    @pl.when((b >= XS) & (b < PLANE))
    def _():
        for copy in plane_sends:
            copy.wait_send()

        @pl.when(b < 2 * XS)
        def _():
            for copy in extra_sends:
                copy.wait_send()


def solution(mesh):
    count = mesh.shape["ctx"]

    def body(queries, cache_keys, cache_values, bounds):
        shape = queries.shape
        size, rows = shape[3], cache_keys.shape[1]
        n = shape[1] * shape[2]
        vmem = pltpu.VMEM
        out = pl.pallas_call(
            lambda *refs: kernel(rows, count, *refs),
            out_shape=jax.ShapeDtypeStruct((n, size), F32),
            in_specs=[pl.BlockSpec(memory_space=pltpu.SMEM)] + [pl.BlockSpec(memory_space=pl.ANY)] * 3,
            out_specs=pl.BlockSpec(memory_space=vmem),
            scratch_shapes=[
                vmem((n, size), F32), vmem((5, rows, size), F32), vmem((5, rows, size), F32),
                vmem((128, size), F32), vmem((128, size), F32),
                vmem((n, 2 * size), BF16), vmem((rows // 2, 2 * size), BF16), vmem((rows // 2, size), BF16),
                vmem((rows // 2, 2 * size), BF16),
                vmem((n, size), F32), vmem((n, size), F32), vmem((n, size), F32),
                pltpu.SemaphoreType.DMA((SINK_SENDS + 20,)), pltpu.SemaphoreType.DMA((SINKS + 2,)),
                pltpu.SemaphoreType.DMA((5,)),
            ],
            compiler_params=pltpu.CompilerParams(collective_id=0, has_side_effects=True),
            name="attend",
        )(bounds.T, queries.reshape(n, size), cache_keys.reshape(rows, size), cache_values.reshape(rows, size))
        return out.reshape(shape)

    in_specs = (P("ctx", None, "kvh", None), P("kvh", "ctx", None), P("kvh", "ctx", None), P())
    return jax.shard_map(body, mesh=mesh, in_specs=in_specs, out_specs=P("ctx", None, "kvh", None), check_vma=False)
```

```python
import math

import jax
import jax.numpy as jnp
from jax import lax
from jax.experimental import pallas as pl
from jax.experimental.pallas import tpu as pltpu
from jax.sharding import PartitionSpec as P

SINK = 64
NEG = -1e30
NT = (((1,), (1,)), ((), ()))
NN = (((1,), (0,)), ((), ()))
F32, BF16 = jnp.float32, jnp.bfloat16
XS = 4
PLANE = 32

NEAR1, TRANSIT, NEAR3, FAR_A, FAR_B, SINKS, RELAY = 0, 4, 8, 12, 16, 20, 22
SINK_SENDS = 26


def split(x):
    high = x.astype(BF16)
    return high, (x - high.astype(F32)).astype(BF16)


def kernel(rows, count, bounds, q_hbm, k_hbm, v_hbm, o_ref, q_raw, kbuf, vbuf, ksink, vsink,
           qcat, kcat, vcat, top, total, mixed, s0, s1, p0, p1, d0, d1, ssem, rsem, lsem,
           wrap_ready, sink_ready):
    scores, weights, decays = (s0, s1), (p0, p1), (d0, d1)
    half, queries, size = rows // 2, q_hbm.shape[0], q_hbm.shape[1]
    b = lax.axis_index("ctx")
    x = lax.rem(b, XS)
    at = lambda d: lax.rem(b + d + count, count)

    def remote(src, dst, send, recv, target):
        return pltpu.make_async_remote_copy(
            src_ref=src, dst_ref=dst, send_sem=ssem.at[send], recv_sem=rsem.at[recv],
            device_id={"ctx": target}, device_id_type=pl.DeviceIdType.MESH)

    local = [
        pltpu.make_async_copy(q_hbm, q_raw, lsem.at[0]),
        pltpu.make_async_copy(k_hbm, kbuf.at[0], lsem.at[1]),
        pltpu.make_async_copy(v_hbm, vbuf.at[0], lsem.at[2]),
    ]
    for copy in local:
        copy.start()

    def signal(sem, target):
        pl.semaphore_signal(sem, inc=1, device_id={"ctx": target}, device_id_type=pl.DeviceIdType.MESH)

    barrier = pltpu.get_barrier_semaphore()
    ys = PLANE // XS - 1
    zs = count // PLANE - 1
    low = lax.rem(b, PLANE)
    sink_source = jnp.where(b < PLANE, x, jnp.where(low < XS, low + XS, low))
    steps = (1, 3, 4)
    for d in steps:
        signal(barrier, at(-d))

        @pl.when(b + d < count)
        def _(d=d):
            signal(barrier, at(d))

    @pl.when(b == 2)
    def _():
        signal(barrier, 0)

    @pl.when(b < XS)
    def _():
        for d in range(1, ys + 1):
            signal(barrier, b + d * XS)

    @pl.when((b >= XS) & (b < PLANE))
    def _():
        for d in range(1, zs + 1):
            signal(barrier, b + d * PLANE)

            @pl.when(b < 2 * XS)
            def _(d=d):
                signal(barrier, b + d * PLANE - XS)

    wraps = sum(jnp.where(b < d, 1, 0) for d in steps)
    extra = jnp.where((b == 0) | (b >= XS), 1, 0)
    pl.semaphore_wait(barrier, 6 - wraps + extra)

    for d in steps:
        @pl.when(b + d >= count)
        def _(d=d):
            signal(wrap_ready, at(d))

    @pl.when(b >= XS)
    def _():
        signal(sink_ready, sink_source)

    def sink_copies(from_input, number, target):
        src = (k_hbm.at[0:SINK], v_hbm.at[0:SINK]) if from_input else (ksink.at[0:SINK], vsink.at[0:SINK])
        dst = (ksink.at[0:SINK], vsink.at[0:SINK])
        return [remote(src[i], dst[i], SINK_SENDS + 2 * number + i, SINKS + i, target) for i in range(2)]

    root_sends = [c for d in range(1, XS) for c in sink_copies(True, d - 1, d)]
    row_sends = [c for d in range(1, ys + 1) for c in sink_copies(True, XS - 2 + d, d * XS)]
    head_sends = [c for d in range(1, ys + 1) for c in sink_copies(False, d - 1, b + d * XS)]
    plane_sends = [c for d in range(1, zs + 1) for c in sink_copies(False, d - 1, b + d * PLANE)]
    extra_sends = [c for d in range(1, zs + 1) for c in sink_copies(False, zs + d - 1, b + d * PLANE - XS)]
    sink_in = [remote(ksink.at[0:SINK], ksink.at[0:SINK], SINK_SENDS, SINKS, at(1)),
               remote(vsink.at[0:SINK], vsink.at[0:SINK], SINK_SENDS, SINKS + 1, at(1))]
    own_sink = [pltpu.make_async_copy(k_hbm.at[0:SINK], ksink.at[0:SINK], lsem.at[3]),
                pltpu.make_async_copy(v_hbm.at[0:SINK], vsink.at[0:SINK], lsem.at[4])]

    @pl.when(b == 0)
    def _():
        for copy in own_sink + root_sends:
            copy.start()

    first, last = x == 0, x == XS - 1
    slot1 = jnp.where(first, 4, 1)
    sem1 = jnp.where(first, TRANSIT, NEAR1)
    target1 = jnp.where(first, at(3), at(-1))
    parts = lambda slot, off: (kbuf.at[slot, pl.ds(off, half)], vbuf.at[slot, pl.ds(off, half)])
    hbm_parts = lambda off: (k_hbm.at[pl.ds(off, half)], v_hbm.at[pl.ds(off, half)])
    near1, near3, relay, far_a, far_b = [], [], [], [], []
    for h in range(2):
        for i in range(2):
            j = 2 * h + i
            off1, off3 = h * half, (1 - h) * half
            near1.append(remote(hbm_parts(off1)[i], parts(slot1, off1)[i], NEAR1 + j, sem1 + j, target1))
            near3.append(remote(hbm_parts(off3)[i], parts(3, off3)[i], NEAR3 + j, NEAR3 + j, at(-3)))
            relay.append(remote(parts(4, off1)[i], parts(1, off1)[i], RELAY + j, NEAR1 + j, at(-4)))
    quarter = half // 2
    for j in range(4):
        buf, off = (kbuf, vbuf)[j % 2], (j // 2) * quarter
        low_rows, high_rows = pl.ds(off, quarter), pl.ds(half + off, quarter)
        far_a.append(remote(buf.at[1, low_rows], buf.at[2, low_rows], FAR_A + j, FAR_A + j, at(-1)))
        far_b.append(remote(buf.at[3, high_rows], buf.at[2, high_rows], FAR_B + j, FAR_B + j, at(1)))
    for j in range(4):
        near1[j].start()

    @pl.when(b >= XS - 1)
    def _():
        for copy in near3:
            copy.start()

    near1_in = [remote(parts(1, (j // 2) * half)[j % 2], parts(1, (j // 2) * half)[j % 2], NEAR1 + j, NEAR1 + j, at(-1))
                for j in range(4)]
    transit_in = [remote(parts(4, (j // 2) * half)[j % 2], parts(4, (j // 2) * half)[j % 2], NEAR1 + j, TRANSIT + j, at(-1))
                  for j in range(4)]

    for copy in local:
        copy.wait()
    scale = math.log2(math.e) / math.sqrt(size)
    step = 256
    lane = lax.broadcasted_iota(jnp.int32, (step, size), 1)

    @pl.loop(0, queries // step)
    def _(i):
        at_rows = pl.ds(pl.multiple_of(i * step, step), step)
        high, rest = split(q_raw[at_rows, :] * scale)
        qcat[at_rows, 0:size] = high
        qcat[at_rows, size:2 * size] = rest
        qcat[at_rows, 2 * size:3 * size] = high
        qcat[at_rows, 3 * size:4 * size] = jnp.where(lane == 0, 1.0, 0.0).astype(BF16)
        top[at_rows, :] = jnp.full((step, size), NEG, F32)
        total[at_rows, :] = jnp.zeros((step, size), F32)
        mixed[at_rows, :] = jnp.zeros((step, size), F32)

    ksink[SINK:, :] = jnp.zeros((half - SINK, size), F32)
    vsink[SINK:, :] = jnp.zeros((half - SINK, size), F32)
    sink_end, lower, upper = bounds[0, b], bounds[1, b], bounds[2, b]
    block = 512
    tiles = queries // block

    def prepare(side, keys, values, seen):
        high, rest = split(keys)
        kcat[side, :, 0:size] = high
        kcat[side, :, size:2 * size] = high
        kcat[side, :, 2 * size:3 * size] = rest
        bias = jnp.where(seen & (lax.broadcasted_iota(jnp.int32, (half, size), 1) == 0), NEG, 0.0)
        kcat[side, :, 3 * size:4 * size] = bias.astype(BF16)
        high, rest = split(values)
        vcat[side, 0:half, 0:size] = high
        vcat[side, 0:half, size:2 * size] = rest
        vcat[side, half:2 * half, 0:size] = high
        vcat[side, half:2 * half, size:2 * size] = rest

    def rows_of(t):
        return pl.ds(pl.multiple_of(lax.rem(t, tiles) * block, block), block)

    def side_of(t):
        return lax.rem(lax.div(t, tiles), 2)

    def score(t, even):
        scores[even][...] = lax.dot_general(qcat[rows_of(t), :], kcat[side_of(t)], NT, preferred_element_type=F32)

    def soften(t, even):
        s = scores[even][...]
        at_rows = rows_of(t)
        before = top[at_rows, :]
        now = jnp.maximum(before, jnp.max(s, axis=1, keepdims=True))
        decay = jnp.exp2(before - now)
        p = jnp.exp2(s - jnp.concatenate([now] * (half // 128), axis=1))
        summed = p[:, 0:128]
        for c in range(1, half // 128):
            summed = summed + p[:, c * 128:(c + 1) * 128]
        high, rest = split(p)
        weights[even][:, 0:half] = high
        weights[even][:, half:2 * half] = rest
        decays[even][...] = decay
        top[at_rows, :] = now
        total[at_rows, :] = total[at_rows, :] * decay + summed

    def mix(t, even):
        out = lax.dot_general(weights[even][...], vcat[side_of(t)], NN, preferred_element_type=F32)
        at_rows = rows_of(t)
        mixed[at_rows, :] = mixed[at_rows, :] * decays[even][...] + (out[:, :size] + out[:, size:])

    def pair(t):
        for u in range(2):
            mix(t + u - 2, u)
            soften(t + u - 1, 1 - u)
            score(t + u, u)

    pieces = 9

    def unseen(offsets):
        return (offsets < lower) | (offsets >= upper)

    slots = lax.broadcasted_iota(jnp.int32, (half, size), 0)
    prepare(0, kbuf[0, 0:half, :], vbuf[0, 0:half, :], unseen(slots))
    score(0, 0)
    score(1, 1)
    soften(0, 0)
    pair(2)

    @pl.loop(1, pieces)
    def _(i):
        slot = jnp.where(i < 2, 0, jnp.where(i > 5, 2, jnp.where(lax.rem(i, 2) == 0, 3, 1)))
        upper_half = (i == 1) | (i == 2) | (i == 5)
        off = pl.multiple_of(jnp.where(upper_half, half, jnp.where(i == 7, quarter, 0)), quarter)
        next_off = pl.multiple_of(off + jnp.where(i > 5, half, quarter), quarter)

        @pl.when((i == 1) & (b < XS - 1))
        def _():
            pl.semaphore_wait(wrap_ready, wraps)
            for copy in near3:
                copy.start()

        @pl.when((i == 1) & (b == 0))
        def _():
            pl.semaphore_wait(sink_ready, ys)
            for copy in row_sends:
                copy.start()

        @pl.when(i == 2)
        def _():
            @pl.when(b == XS - 1)
            def _():
                pl.semaphore_wait(wrap_ready, 1)

            @pl.when(last)
            def _():
                transit_in[0].wait_recv()
                relay[0].start()

            for j in range(2):
                near3[j].wait_recv()
            for copy in far_b:
                copy.start()

            @pl.when(last)
            def _():
                transit_in[1].wait_recv()
                relay[1].start()

            @pl.when((b > 0) & (b < XS))
            def _():
                for copy in sink_in:
                    copy.wait_recv()
                pl.semaphore_wait(sink_ready, ys)
                for copy in head_sends:
                    copy.start()

        @pl.when(i == 3)
        def _():
            @pl.when(last)
            def _():
                for j in range(2, 4):
                    transit_in[j].wait_recv()
                    relay[j].start()

            for j in range(2):
                near1_in[j].wait_recv()
            for copy in far_a:
                copy.start()

        @pl.when(i == 4)
        def _():
            for j in range(2, 4):
                near3[j].wait_recv()

        @pl.when(i == 5)
        def _():
            for j in range(2, 4):
                near1_in[j].wait_recv()

        row = lax.div(b, XS)
        turn = jnp.where(row == 1, 4, 5)

        @pl.when((i == turn) & (b >= XS) & (b < PLANE))
        def _():
            for copy in sink_in:
                copy.wait_recv()
            pl.semaphore_wait(sink_ready, jnp.where(row == 1, 2 * zs, zs))
            for copy in plane_sends:
                copy.start()

            @pl.when(row == 1)
            def _():
                for copy in extra_sends:
                    copy.start()

        @pl.when(i == 6)
        def _():
            for j in range(2):
                far_b[j].wait_recv()
                far_a[j].wait_recv()

        @pl.when(i == 7)
        def _():
            for j in range(2, 4):
                far_b[j].wait_recv()
                far_a[j].wait_recv()

        @pl.when(i < pieces - 1)
        def _():
            both = lambda buf: jnp.concatenate(
                [buf[slot, pl.ds(off, quarter), :], buf[slot, pl.ds(next_off, quarter), :]], axis=0)
            offsets = slot * rows + slots + jnp.where(slots < quarter, off, next_off - quarter)
            prepare(lax.rem(i, 2), both(kbuf), both(vbuf), unseen(offsets))

        @pl.when(i == pieces - 1)
        def _():
            @pl.when(b == 0)
            def _():
                for copy in own_sink:
                    copy.wait()

            @pl.when(b >= PLANE)
            def _():
                for copy in sink_in:
                    copy.wait_recv()

            place = slots - b * rows
            place = jnp.where(place < 0, place + rows * count, place)
            prepare((pieces - 1) % 2, ksink[...], vsink[...], (slots >= sink_end) | jnp.logical_not(unseen(place)))

        @pl.loop(0, tiles // 2)
        def _(c):
            pair(i * tiles + 2 * c)

    last_tile = pieces * tiles - 1
    mix(last_tile - 1, 0)
    soften(last_tile, 1)
    mix(last_tile, 1)

    @pl.loop(0, queries // step)
    def _(i):
        at_rows = pl.ds(pl.multiple_of(i * step, step), step)
        o_ref[at_rows, :] = mixed[at_rows, :] / jnp.sum(total[at_rows, :], axis=1, keepdims=True)

    for copy in near1 + near3 + far_a + far_b:
        copy.wait_send()

    @pl.when(last)
    def _():
        for copy in relay:
            copy.wait_send()

    @pl.when(b == 0)
    def _():
        for copy in root_sends + row_sends:
            copy.wait_send()

    @pl.when((b > 0) & (b < XS))
    def _():
        for copy in head_sends:
            copy.wait_send()

    @pl.when((b >= XS) & (b < PLANE))
    def _():
        for copy in plane_sends:
            copy.wait_send()

        @pl.when(b < 2 * XS)
        def _():
            for copy in extra_sends:
                copy.wait_send()


def solution(mesh):
    count = mesh.shape["ctx"]

    def body(queries, cache_keys, cache_values, bounds):
        shape = queries.shape
        size, rows = shape[3], cache_keys.shape[1]
        n = shape[1] * shape[2]
        vmem = pltpu.VMEM
        out = pl.pallas_call(
            lambda *refs: kernel(rows, count, *refs),
            out_shape=vmem((n, size), F32),
            in_specs=[pl.BlockSpec(memory_space=pltpu.SMEM)] + [pl.BlockSpec(memory_space=pl.ANY)] * 3,
            out_specs=pl.BlockSpec(memory_space=vmem),
            scratch_shapes=[
                vmem((n, size), F32), vmem((5, rows, size), F32), vmem((5, rows, size), F32),
                vmem((rows // 2, size), F32), vmem((rows // 2, size), F32),
                vmem((n, 4 * size), BF16), vmem((2, rows // 2, 4 * size), BF16), vmem((2, rows, 2 * size), BF16),
                vmem((n, size), F32), vmem((n, size), F32), vmem((n, size), F32),
                vmem((512, rows // 2), F32), vmem((512, rows // 2), F32),
                vmem((512, rows), BF16), vmem((512, rows), BF16), vmem((512, size), F32), vmem((512, size), F32),
                pltpu.SemaphoreType.DMA((SINK_SENDS + 20,)), pltpu.SemaphoreType.DMA((SINKS + 2,)),
                pltpu.SemaphoreType.DMA((5,)), pltpu.SemaphoreType.REGULAR, pltpu.SemaphoreType.REGULAR,
            ],
            compiler_params=pltpu.CompilerParams(collective_id=0, has_side_effects=True),
            name="attend",
        )(bounds.T, queries.reshape(n, size), cache_keys.reshape(rows, size), cache_values.reshape(rows, size))
        return out.reshape(shape)

    in_specs = (P("ctx", None, "kvh", None), P("kvh", "ctx", None), P("kvh", "ctx", None), P())
    return jax.shard_map(body, mesh=mesh, in_specs=in_specs, out_specs=P("ctx", None, "kvh", None), check_vma=False)
```

```python
import math

import jax
import jax.numpy as jnp
from jax import lax
from jax.experimental import pallas as pl
from jax.experimental.pallas import tpu as pltpu
from jax.sharding import PartitionSpec as P

SINK = 64
NEG = -1e30
NT = (((1,), (1,)), ((), ()))
NN = (((1,), (0,)), ((), ()))
F32, BF16 = jnp.float32, jnp.bfloat16
XS = 4
PLANE = 32

NEAR1, TRANSIT, NEAR3, FAR_A, FAR_B, SINKS, RELAY = 0, 4, 8, 12, 16, 20, 22
SINK_SENDS = 26


def split(x):
    high = x.astype(BF16)
    return high, (x - high.astype(F32)).astype(BF16)


def kernel(rows, count, bounds, q_hbm, k_hbm, v_hbm, o_ref, q_raw, kbuf, vbuf, ksink, vsink,
           qcat, kcat, vcat, top, total, mixed, s0, s1, p0, p1, d0, d1, ssem, rsem, lsem,
           wrap_ready, sink_ready):
    scores, weights, decays = (s0, s1), (p0, p1), (d0, d1)
    half, queries, size = rows // 2, q_hbm.shape[0], q_hbm.shape[1]
    b = lax.axis_index("ctx")
    x = lax.rem(b, XS)
    at = lambda d: lax.rem(b + d + count, count)

    def remote(src, dst, send, recv, target):
        return pltpu.make_async_remote_copy(
            src_ref=src, dst_ref=dst, send_sem=ssem.at[send], recv_sem=rsem.at[recv],
            device_id={"ctx": target}, device_id_type=pl.DeviceIdType.MESH)

    local = [
        pltpu.make_async_copy(q_hbm, q_raw, lsem.at[0]),
        pltpu.make_async_copy(k_hbm, kbuf.at[0], lsem.at[1]),
        pltpu.make_async_copy(v_hbm, vbuf.at[0], lsem.at[2]),
    ]
    for copy in local:
        copy.start()

    def signal(sem, target):
        pl.semaphore_signal(sem, inc=1, device_id={"ctx": target}, device_id_type=pl.DeviceIdType.MESH)

    barrier = pltpu.get_barrier_semaphore()
    ys = PLANE // XS - 1
    zs = count // PLANE - 1
    low = lax.rem(b, PLANE)
    mid_row = PLANE // XS // 2
    mid = mid_row * XS
    sink_source = jnp.where(b < PLANE, jnp.where((x == 0) & (b > mid), mid, x), jnp.where(low < XS, low + XS, low))
    steps = (1, 3, 4)
    for d in steps:
        signal(barrier, at(-d))

        @pl.when(b + d < count)
        def _(d=d):
            signal(barrier, at(d))

    @pl.when(b == 2)
    def _():
        signal(barrier, 0)

    @pl.when(b < XS)
    def _():
        for d in range(1, ys + 1):
            @pl.when((b > 0) | (d <= mid_row))
            def _(d=d):
                signal(barrier, b + d * XS)

    @pl.when(b == mid)
    def _():
        for d in range(1, ys - mid_row + 1):
            signal(barrier, b + d * XS)

    @pl.when((b >= XS) & (b < PLANE))
    def _():
        for d in range(1, zs + 1):
            signal(barrier, b + d * PLANE)

            @pl.when(b < 2 * XS)
            def _(d=d):
                signal(barrier, b + d * PLANE - XS)

    wraps = sum(jnp.where(b < d, 1, 0) for d in steps)
    extra = jnp.where((b == 0) | (b >= XS), 1, 0)
    pl.semaphore_wait(barrier, 6 - wraps + extra)

    for d in steps:
        @pl.when(b + d >= count)
        def _(d=d):
            signal(wrap_ready, at(d))

    @pl.when(b >= XS)
    def _():
        signal(sink_ready, sink_source)

    def sink_copies(from_input, number, target):
        src = (k_hbm.at[0:SINK], v_hbm.at[0:SINK]) if from_input else (ksink.at[0:SINK], vsink.at[0:SINK])
        dst = (ksink.at[0:SINK], vsink.at[0:SINK])
        return [remote(src[i], dst[i], SINK_SENDS + 2 * number + i, SINKS + i, target) for i in range(2)]

    root_sends = [c for d in range(1, XS) for c in sink_copies(True, d - 1, d)]
    row_sends = [c for d in range(mid_row, 0, -1) for c in sink_copies(True, XS - 2 + d, d * XS)]
    mid_sends = [c for d in range(1, ys - mid_row + 1) for c in sink_copies(False, 2 * zs + d - 1, b + d * XS)]
    head_sends = [c for d in range(1, ys + 1) for c in sink_copies(False, d - 1, b + d * XS)]
    plane_sends = [c for d in range(1, zs + 1) for c in sink_copies(False, d - 1, b + d * PLANE)]
    extra_sends = [c for d in range(1, zs + 1) for c in sink_copies(False, zs + d - 1, b + d * PLANE - XS)]
    sink_in = [remote(ksink.at[0:SINK], ksink.at[0:SINK], SINK_SENDS, SINKS, at(1)),
               remote(vsink.at[0:SINK], vsink.at[0:SINK], SINK_SENDS, SINKS + 1, at(1))]
    own_sink = [pltpu.make_async_copy(k_hbm.at[0:SINK], ksink.at[0:SINK], lsem.at[3]),
                pltpu.make_async_copy(v_hbm.at[0:SINK], vsink.at[0:SINK], lsem.at[4])]

    @pl.when(b == 0)
    def _():
        for copy in own_sink + root_sends:
            copy.start()

    first, last = x == 0, x == XS - 1
    slot1 = jnp.where(first, 4, 1)
    sem1 = jnp.where(first, TRANSIT, NEAR1)
    target1 = jnp.where(first, at(3), at(-1))
    parts = lambda slot, off: (kbuf.at[slot, pl.ds(off, half)], vbuf.at[slot, pl.ds(off, half)])
    hbm_parts = lambda off: (k_hbm.at[pl.ds(off, half)], v_hbm.at[pl.ds(off, half)])
    near1, near3, relay, far_a, far_b = [], [], [], [], []
    for h in range(2):
        for i in range(2):
            j = 2 * h + i
            off1, off3 = h * half, (1 - h) * half
            near1.append(remote(hbm_parts(off1)[i], parts(slot1, off1)[i], NEAR1 + j, sem1 + j, target1))
            near3.append(remote(hbm_parts(off3)[i], parts(3, off3)[i], NEAR3 + j, NEAR3 + j, at(-3)))
            relay.append(remote(parts(4, off1)[i], parts(1, off1)[i], RELAY + j, NEAR1 + j, at(-4)))
    quarter = half // 2
    for j in range(4):
        buf, off = (kbuf, vbuf)[j % 2], (j // 2) * quarter
        low_rows, high_rows = pl.ds(off, quarter), pl.ds(half + off, quarter)
        far_a.append(remote(buf.at[1, low_rows], buf.at[2, low_rows], FAR_A + j, FAR_A + j, at(-1)))
        far_b.append(remote(buf.at[3, high_rows], buf.at[2, high_rows], FAR_B + j, FAR_B + j, at(1)))
    for j in range(4):
        near1[j].start()

    @pl.when(b >= XS - 1)
    def _():
        for copy in near3:
            copy.start()

    near1_in = [remote(parts(1, (j // 2) * half)[j % 2], parts(1, (j // 2) * half)[j % 2], NEAR1 + j, NEAR1 + j, at(-1))
                for j in range(4)]
    transit_in = [remote(parts(4, (j // 2) * half)[j % 2], parts(4, (j // 2) * half)[j % 2], NEAR1 + j, TRANSIT + j, at(-1))
                  for j in range(4)]

    for copy in local:
        copy.wait()
    scale = math.log2(math.e) / math.sqrt(size)
    step = 256
    lane = lax.broadcasted_iota(jnp.int32, (step, size), 1)

    @pl.loop(0, queries // step)
    def _(i):
        at_rows = pl.ds(pl.multiple_of(i * step, step), step)
        high, rest = split(q_raw[at_rows, :] * scale)
        qcat[at_rows, 0:size] = high
        qcat[at_rows, size:2 * size] = rest
        qcat[at_rows, 2 * size:3 * size] = high
        qcat[at_rows, 3 * size:4 * size] = jnp.where(lane == 0, 1.0, 0.0).astype(BF16)
        top[at_rows, :] = jnp.full((step, size), NEG, F32)
        total[at_rows, :] = jnp.zeros((step, size), F32)
        mixed[at_rows, :] = jnp.zeros((step, size), F32)

    ksink[SINK:, :] = jnp.zeros((half - SINK, size), F32)
    vsink[SINK:, :] = jnp.zeros((half - SINK, size), F32)
    sink_end, lower, upper = bounds[0, b], bounds[1, b], bounds[2, b]
    block = 512
    tiles = queries // block

    def prepare(side, keys, values, seen):
        high, rest = split(keys)
        kcat[side, :, 0:size] = high
        kcat[side, :, size:2 * size] = high
        kcat[side, :, 2 * size:3 * size] = rest
        bias = jnp.where(seen & (lax.broadcasted_iota(jnp.int32, (half, size), 1) == 0), NEG, 0.0)
        kcat[side, :, 3 * size:4 * size] = bias.astype(BF16)
        high, rest = split(values)
        vcat[side, 0:half, 0:size] = high
        vcat[side, 0:half, size:2 * size] = rest
        vcat[side, half:2 * half, 0:size] = high
        vcat[side, half:2 * half, size:2 * size] = rest

    def rows_of(t):
        return pl.ds(pl.multiple_of(lax.rem(t, tiles) * block, block), block)

    def side_of(t):
        return lax.rem(lax.div(t, tiles), 2)

    def score(t, even):
        scores[even][...] = lax.dot_general(qcat[rows_of(t), :], kcat[side_of(t)], NT, preferred_element_type=F32)

    def soften(t, even):
        s = scores[even][...]
        at_rows = rows_of(t)
        before = top[at_rows, :]
        now = jnp.maximum(before, jnp.max(s, axis=1, keepdims=True))
        decay = jnp.exp2(before - now)
        p = jnp.exp2(s - jnp.concatenate([now] * (half // 128), axis=1))
        summed = p[:, 0:128]
        for c in range(1, half // 128):
            summed = summed + p[:, c * 128:(c + 1) * 128]
        high, rest = split(p)
        weights[even][:, 0:half] = high
        weights[even][:, half:2 * half] = rest
        decays[even][...] = decay
        top[at_rows, :] = now
        total[at_rows, :] = total[at_rows, :] * decay + summed

    def mix(t, even):
        out = lax.dot_general(weights[even][...], vcat[side_of(t)], NN, preferred_element_type=F32)
        at_rows = rows_of(t)
        mixed[at_rows, :] = mixed[at_rows, :] * decays[even][...] + (out[:, :size] + out[:, size:])

    def pair(t):
        for u in range(2):
            mix(t + u - 2, u)
            soften(t + u - 1, 1 - u)
            score(t + u, u)

    pieces = 9

    def unseen(offsets):
        return (offsets < lower) | (offsets >= upper)

    slots = lax.broadcasted_iota(jnp.int32, (half, size), 0)
    prepare(0, kbuf[0, 0:half, :], vbuf[0, 0:half, :], unseen(slots))
    score(0, 0)
    score(1, 1)
    soften(0, 0)
    pair(2)

    @pl.loop(1, pieces)
    def _(i):
        k = jnp.where(b == 0, jnp.where(i == 5, 8, jnp.where(i == 7, 5, jnp.where(i == 8, 7, i))), i)
        far = (k == 5) | (k == 7)
        slot = jnp.where(k < 2, 0, jnp.where(far, 2, jnp.where((k == 2) | (k == 6), 3, 1)))
        upper_half = (k == 1) | (k == 2) | (k == 4)
        off = pl.multiple_of(jnp.where(upper_half, half, jnp.where(k == 7, quarter, 0)), quarter)
        next_off = pl.multiple_of(off + jnp.where(far, half, quarter), quarter)

        @pl.when((i == 1) & (b == 0))
        def _():
            pl.semaphore_wait(sink_ready, mid_row)
            for copy in row_sends:
                copy.start()

        @pl.when((i == 1) & (b < XS - 1))
        def _():
            pl.semaphore_wait(wrap_ready, wraps)
            for copy in near3:
                copy.start()

        @pl.when(i == 2)
        def _():
            @pl.when(b == XS - 1)
            def _():
                pl.semaphore_wait(wrap_ready, 1)

            @pl.when(last)
            def _():
                transit_in[0].wait_recv()
                relay[0].start()

            for j in range(2):
                near3[j].wait_recv()
            for copy in far_b:
                copy.start()

            @pl.when(last)
            def _():
                transit_in[1].wait_recv()
                relay[1].start()

            @pl.when((b > 0) & (b < XS))
            def _():
                for copy in sink_in:
                    copy.wait_recv()
                pl.semaphore_wait(sink_ready, ys)
                for copy in head_sends:
                    copy.start()

        @pl.when(i == 3)
        def _():
            @pl.when(last)
            def _():
                for j in range(2, 4):
                    transit_in[j].wait_recv()
                    relay[j].start()

            for j in range(2):
                near1_in[j].wait_recv()
            for copy in far_a:
                copy.start()

            @pl.when(b == mid)
            def _():
                for copy in sink_in:
                    copy.wait_recv()
                pl.semaphore_wait(sink_ready, ys - mid_row + zs)
                for copy in mid_sends:
                    copy.start()

        row = lax.div(b, XS)

        @pl.when((i == jnp.where(row == 1, 4, 5)) & (b >= XS) & (b < PLANE))
        def _():
            @pl.when(b != mid)
            def _():
                for copy in sink_in:
                    copy.wait_recv()
                pl.semaphore_wait(sink_ready, jnp.where(row == 1, 2 * zs, zs))

            for copy in plane_sends:
                copy.start()

            @pl.when(row == 1)
            def _():
                for copy in extra_sends:
                    copy.start()

        @pl.when(i == 4)
        def _():
            for j in range(2, 4):
                near1_in[j].wait_recv()

        @pl.when(k == 5)
        def _():
            for j in range(2):
                far_b[j].wait_recv()
                far_a[j].wait_recv()

        @pl.when(k == 6)
        def _():
            for j in range(2, 4):
                near3[j].wait_recv()

        @pl.when(k == 7)
        def _():
            for j in range(2, 4):
                far_b[j].wait_recv()
                far_a[j].wait_recv()

        @pl.when(k < pieces - 1)
        def _():
            both = lambda buf: jnp.concatenate(
                [buf[slot, pl.ds(off, quarter), :], buf[slot, pl.ds(next_off, quarter), :]], axis=0)
            offsets = slot * rows + slots + jnp.where(slots < quarter, off, next_off - quarter)
            prepare(lax.rem(i, 2), both(kbuf), both(vbuf), unseen(offsets))

        @pl.when(k == pieces - 1)
        def _():
            @pl.when(b == 0)
            def _():
                for copy in own_sink:
                    copy.wait()

            @pl.when(b >= PLANE)
            def _():
                for copy in sink_in:
                    copy.wait_recv()

            place = slots - b * rows
            place = jnp.where(place < 0, place + rows * count, place)
            prepare(lax.rem(i, 2), ksink[...], vsink[...], (slots >= sink_end) | jnp.logical_not(unseen(place)))

        @pl.loop(0, tiles // 2)
        def _(c):
            pair(i * tiles + 2 * c)

    last_tile = pieces * tiles - 1
    mix(last_tile - 1, 0)
    soften(last_tile, 1)
    mix(last_tile, 1)

    @pl.loop(0, queries // step)
    def _(i):
        at_rows = pl.ds(pl.multiple_of(i * step, step), step)
        o_ref[at_rows, :] = mixed[at_rows, :] / jnp.sum(total[at_rows, :], axis=1, keepdims=True)

    for copy in near1 + near3 + far_a + far_b:
        copy.wait_send()

    @pl.when(last)
    def _():
        for copy in relay:
            copy.wait_send()

    @pl.when(b == 0)
    def _():
        for copy in root_sends + row_sends:
            copy.wait_send()

    @pl.when(b == mid)
    def _():
        for copy in mid_sends:
            copy.wait_send()

    @pl.when((b > 0) & (b < XS))
    def _():
        for copy in head_sends:
            copy.wait_send()

    @pl.when((b >= XS) & (b < PLANE))
    def _():
        for copy in plane_sends:
            copy.wait_send()

        @pl.when(b < 2 * XS)
        def _():
            for copy in extra_sends:
                copy.wait_send()


def solution(mesh):
    count = mesh.shape["ctx"]

    def body(queries, cache_keys, cache_values, bounds):
        shape = queries.shape
        size, rows = shape[3], cache_keys.shape[1]
        n = shape[1] * shape[2]
        vmem = pltpu.VMEM
        out = pl.pallas_call(
            lambda *refs: kernel(rows, count, *refs),
            out_shape=vmem((n, size), F32),
            in_specs=[pl.BlockSpec(memory_space=pltpu.SMEM)] + [pl.BlockSpec(memory_space=pl.ANY)] * 3,
            out_specs=pl.BlockSpec(memory_space=vmem),
            scratch_shapes=[
                vmem((n, size), F32), vmem((5, rows, size), F32), vmem((5, rows, size), F32),
                vmem((rows // 2, size), F32), vmem((rows // 2, size), F32),
                vmem((n, 4 * size), BF16), vmem((2, rows // 2, 4 * size), BF16), vmem((2, rows, 2 * size), BF16),
                vmem((n, size), F32), vmem((n, size), F32), vmem((n, size), F32),
                vmem((512, rows // 2), F32), vmem((512, rows // 2), F32),
                vmem((512, rows), BF16), vmem((512, rows), BF16), vmem((512, size), F32), vmem((512, size), F32),
                pltpu.SemaphoreType.DMA((SINK_SENDS + 20,)), pltpu.SemaphoreType.DMA((SINKS + 2,)),
                pltpu.SemaphoreType.DMA((5,)), pltpu.SemaphoreType.REGULAR, pltpu.SemaphoreType.REGULAR,
            ],
            compiler_params=pltpu.CompilerParams(collective_id=0, has_side_effects=True),
            name="attend",
        )(bounds.T, queries.reshape(n, size), cache_keys.reshape(rows, size), cache_values.reshape(rows, size))
        return out.reshape(shape)

    in_specs = (P("ctx", None, "kvh", None), P("kvh", "ctx", None), P("kvh", "ctx", None), P())
    return jax.shard_map(body, mesh=mesh, in_specs=in_specs, out_specs=P("ctx", None, "kvh", None), check_vma=False)
```
